128 devices in a mesh: seq: 16 (over x, y), exp: 8 (over z, core).
Axes of the slice: x: 4, y: 4, z: 4, core: 2. Of those that a mesh axis runs over, the one named last changes fastest.
Arguments:
- upstream: bfloat16 [8192, 6144], P(('seq', 'exp')), may hold values from -6 to 6
- out_weight: bfloat16 [4096, 6144], P('exp'), may hold values from -0.078125 to 0.078125
- queries: bfloat16 [8192, 4096], P('seq', 'exp'), may hold values from -6 to 6
- keys: bfloat16 [8192, 4096], P('seq', 'exp'), may hold values from -6 to 6
- values: bfloat16 [8192, 4096], P('seq', 'exp'), may hold values from -6 to 6
- log_decay: float32 [32, 8192], P('exp', 'seq'), may hold values from -0.8 to 0, as said below
- expert_ids: int32 [8192, 2], P(('seq', 'exp')), may hold values from 0 to 15, all different within a row; in each aligned block of 64 rows (0 to 63, 64 to 127, ...) at most 9 rows name the same one
- gate_probs: float32 [8192, 2], P(('seq', 'exp')), may hold values from 0.05 to 0.95
- activations: bfloat16 [16, 4608, 1152], P('exp', 'seq'), may hold values from -1.5 to 1.5
Outputs:
- d_queries: bfloat16 [8192, 4096], P('seq', 'exp')
- d_keys: bfloat16 [8192, 4096], P('seq', 'exp')
- d_values: bfloat16 [8192, 4096], P('seq', 'exp')
- d_down: bfloat16 [16, 4608, 6144], P('exp', 'seq')
The draws below stay inside these ranges and needn't reach their ends.
Inputs may be any that keep to these rules, and one draw needn't show every extreme that they name: `expert_ids`: each row names two different experts. In every block of 64 rows no expert is named more than 9 times, and in every draw some block names some expert exactly 9 times. `log_decay`: negative at every position.
All inputs are finite; a program needn't handle non-finite values.
Results may differ from the reference program's by a relative error of at most 0.005.
Values may be sent and summed in bfloat16 or wider, within the bound.
A program may use at most 192 MiB of HBM per device.

```python
import math
import jax
import jax.numpy as jnp
import numpy as np
from jax import lax

D = 6144
HEAD = 128
ATTENTION_HEADS = 32
EXPERTS = 16
FF = 4608
TOK_SEQ = 512
SEQUENCE_TOKENS = 8192
TOK_DEV = 64
MOST = 9
SLOTS = 1152
N_SEQ = 16
N_EXP = 8


def draw_log_decay(key, part):
    key_sequence = jax.random.split(key, 6)
    slow_share = 0.5
    shuffled = jax.random.permutation(key_sequence[0], ATTENTION_HEADS)
    slow_heads = (shuffled.astype(jnp.float32) < slow_share * ATTENTION_HEADS)[:, None]
    slow_rate = 0.3 / SEQUENCE_TOKENS * jnp.exp(jax.random.uniform(key_sequence[1], (ATTENTION_HEADS, 1), minval=0.0, maxval=0.69))
    fast_rate = jnp.exp(jax.random.uniform(key_sequence[2], (ATTENTION_HEADS, 1), minval=jnp.log(1.0 / 50.0), maxval=jnp.log(1.0 / 30.0)))
    per_head_decay_rate = jnp.where(slow_heads, slow_rate, fast_rate)
    noise_level = jnp.exp(jax.random.uniform(key_sequence[3], (ATTENTION_HEADS, SEQUENCE_TOKENS), minval=-0.7, maxval=0.7))
    spike_positions = jax.random.randint(key_sequence[4], (2,), 0, SEQUENCE_TOKENS)
    spike_mask = jnp.any(jnp.arange(SEQUENCE_TOKENS)[:, None] == spike_positions[None, :], axis=1)
    spike_dropout = jnp.log(jax.random.uniform(key_sequence[5], (ATTENTION_HEADS, 1), minval=0.5, maxval=0.8))
    return (-per_head_decay_rate * noise_level + jnp.where(spike_mask[None, :], spike_dropout, 0.0)).astype(jnp.float32)


def block_scale(own_key, dims, pieces, smallest, largest):
    gain = 1.0
    for dim, blocks in pieces:
        draws = jax.random.uniform(jax.random.fold_in(jax.random.fold_in(own_key, 6), dim), (blocks,), jnp.float32, smallest / len(pieces), largest / len(pieces))
        gain = gain * jnp.repeat(jnp.exp(draws), dims[dim] // blocks).reshape((-1,) + (1,) * (len(dims) - 1 - dim))
    return gain


def routed_block(rng, own, number, rows, amount, top, limit, lean):
    order = jax.random.permutation(rng, amount)
    packed, ordinary = portions_of(amount, rows * top, limit, lean, True), portions_of(amount, rows * top, limit, lean, False)
    places = jnp.arange(amount)

    def named(sizes, turn):
        used = int((sizes > 0).sum())
        fixed = max(1, used // 4)
        shifted = fixed + (places - fixed + turn * (used - fixed)) % max(1, amount - fixed)
        return jnp.zeros((amount,), jnp.int32).at[order[jnp.where(places < fixed, places, shifted)]].set(jnp.asarray(sizes, jnp.int32))

    sizes = jnp.where(number % 4 == 0, named(packed, number // 4), named(ordinary, number - number // 4 - 1))
    mixed = jax.random.permutation(jax.random.fold_in(own, 3), amount)
    giver, sink = mixed[0:amount // 2 * 2:2], mixed[1:amount // 2 * 2:2]
    margin = jnp.minimum(sizes[giver] - 1, limit - sizes[sink]) // 2
    margin = jnp.where((giver == order[0]) | (sink == order[0]) | (sizes[sink] == 0), 0, jnp.maximum(margin, 0))
    shifted = jax.random.randint(jax.random.fold_in(own, 4), (amount // 2,), 0, 1 << 20) % (margin + 1)
    sizes = sizes.at[giver].add(-shifted).at[sink].add(shifted)
    items = jnp.searchsorted(jnp.cumsum(sizes), jnp.arange(rows * top), side="right").astype(jnp.int32)
    table = items.reshape(top, rows).T
    table = table[jax.random.permutation(jax.random.fold_in(own, 1), rows)]
    turn = jax.random.randint(jax.random.fold_in(own, 2), (rows, 1), 0, top)
    return jnp.take_along_axis(table, (jnp.arange(top)[None, :] + turn) % top, axis=1)


def portions_of(amount, total, limit, lean, full):
    weights = [(1 << 20) // math.isqrt(grade ** lean) + 1 for grade in range(1, amount + 1)]
    largest = limit if full else min(limit, max(-(-total // amount), total * weights[0] // sum(weights)))
    least = 1 if total - largest >= amount - 1 else 0
    holding, surplus = [largest] + [least] * (amount - 1), total - largest - least * (amount - 1)
    while surplus > 0:
        candidates = [i for i in range(1, amount) if holding[i] < largest] or [i for i in range(1, amount) if holding[i] < limit]
        pool, budget = sum([weights[i] for i in candidates]), surplus
        for i in candidates:
            extra = min(limit - holding[i], max(1, budget * weights[i] // pool), surplus)
            holding[i] = holding[i] + extra
            surplus = surplus - extra
    return np.array(holding)


def gaussian(own_key, dims, scale, most, cuts=(), kind=jnp.bfloat16):
    factor_of = block_scale(own_key, dims, cuts, -0.22, 0.18) if cuts else 1.0
    values = jax.random.normal(own_key, dims, jnp.float32) * scale * factor_of
    return jnp.minimum(jnp.maximum(values, -most), most).astype(kind)


def setup_inputs(seed: int = 0) -> dict:
    seeds = jax.random.split(jax.random.key(seed), 10)
    upstream = gaussian(seeds[0], (SEQUENCE_TOKENS, D), 1.0, 6.0, ((0, 128),))
    out_weight = gaussian(seeds[1], (ATTENTION_HEADS * HEAD, D), D ** -0.5, 0.078125, ((0, 8),))
    queries = gaussian(seeds[2], (SEQUENCE_TOKENS, ATTENTION_HEADS * HEAD), 1.0, 6.0, ((0, 16), (1, 8)))
    keys = gaussian(seeds[3], (SEQUENCE_TOKENS, ATTENTION_HEADS * HEAD), 1.0, 6.0, ((0, 16), (1, 8)))
    values = gaussian(seeds[4], (SEQUENCE_TOKENS, ATTENTION_HEADS * HEAD), 1.0, 6.0, ((0, 16), (1, 8)))
    log_decay = draw_log_decay(jax.random.fold_in(seeds[9], 71), 0)
    expert_ids_keys = jax.random.split(jax.random.fold_in(seeds[6], 1), SEQUENCE_TOKENS // TOK_DEV)
    expert_ids_turns = jax.random.permutation(jax.random.fold_in(seeds[6], 3), SEQUENCE_TOKENS // TOK_DEV)
    expert_ids = jax.vmap(lambda own, number: routed_block(jax.random.fold_in(seeds[6], 2), own, number, TOK_DEV, EXPERTS, 2, MOST, 2))(expert_ids_keys, expert_ids_turns).reshape((SEQUENCE_TOKENS, 2))
    gate_probs = jnp.clip(0.05 + 0.9 * jax.random.uniform(seeds[7], (SEQUENCE_TOKENS, 2), jnp.float32) ** block_scale(seeds[7], (SEQUENCE_TOKENS, 2), ((0, 128),), -0.2, 0.2), 0.05, 0.95)
    activations = gaussian(seeds[8], (EXPERTS, FF, SLOTS), 0.25, 1.5, ((0, 8), (1, 16)))
    return {"upstream": upstream, "out_weight": out_weight, "queries": queries, "keys": keys, "values": values, "log_decay": log_decay, "expert_ids": expert_ids, "gate_probs": gate_probs, "activations": activations}


HIGH = lax.Precision.HIGHEST

def decay_factors(cumulative):
    lead = jnp.exp(cumulative).T[:, :, None]
    tail = jnp.exp(cumulative[:, -1:] - cumulative).T[:, :, None]
    return (lead, tail)

def block_terms(query_heads, key_heads, value_heads, grad_heads, cumulative, lead, tail, state_in, adjoint_in):
    length = cumulative.shape[1]
    position = jnp.arange(length)
    lower = position[:, None] >= position[None, :]
    spread = cumulative[:, :, None] - cumulative[:, None, :]
    weights = jnp.where(lower[None], jnp.exp(jnp.minimum(spread, 0.0)), 0.0)
    mixed = jnp.einsum('thf,shf->hts', grad_heads, value_heads, precision=HIGH) * weights
    paired = jnp.einsum('the,she->hts', query_heads, key_heads, precision=HIGH) * weights
    d_query = jnp.einsum('hts,she->the', mixed, key_heads, precision=HIGH) + lead * jnp.einsum('thf,hef->the', grad_heads, state_in, precision=HIGH)
    d_key = jnp.einsum('hts,the->she', mixed, query_heads, precision=HIGH) + tail * jnp.einsum('shf,hef->she', value_heads, adjoint_in, precision=HIGH)
    d_value = jnp.einsum('hts,thf->shf', paired, grad_heads, precision=HIGH) + tail * jnp.einsum('she,hef->shf', key_heads, adjoint_in, precision=HIGH)
    return (d_query, d_key, d_value)

def reference(upstream, out_weight, queries, keys, values, log_decay, expert_ids, gate_probs, activations):
    grad_out = jnp.dot(upstream, out_weight.T, preferred_element_type=jnp.float32).astype(jnp.bfloat16)
    blocks = SEQUENCE_TOKENS // TOK_SEQ
    scale = 1.0 / math.sqrt(HEAD * SEQUENCE_TOKENS)

    def split_heads(block):
        return block.astype(jnp.float32).reshape(blocks, TOK_SEQ, ATTENTION_HEADS, HEAD)
    query_heads = split_heads(queries)
    key_heads = split_heads(keys)
    value_heads = split_heads(values)
    grad_heads = split_heads(grad_out)
    cumulative = jnp.cumsum(log_decay.reshape(ATTENTION_HEADS, blocks, TOK_SEQ).transpose(1, 0, 2), axis=2)

    def summarize(items):
        query_block, key_block, value_block, grad_block, cumul_block = items
        lead, tail = decay_factors(cumul_block)
        kv_sum = jnp.einsum('she,shf->hef', key_block * tail, value_block, precision=HIGH)
        qo_sum = jnp.einsum('the,thf->hef', query_block * lead, grad_block, precision=HIGH)
        return (cumul_block[:, -1], kv_sum, qo_sum)
    totals, kv_sums, qo_sums = lax.map(summarize, (query_heads, key_heads, value_heads, grad_heads, cumulative))
    zero_state = jnp.zeros((ATTENTION_HEADS, HEAD, HEAD), jnp.float32)

    def forward(carry, item):
        total, kv_sum = item
        return (jnp.exp(total)[:, None, None] * carry + kv_sum, carry)

    def backward(carry, item):
        total, qo_sum = item
        return (qo_sum + jnp.exp(total)[:, None, None] * carry, carry)
    _, states_in = lax.scan(forward, zero_state, (totals, kv_sums))
    _, adjoints_in = lax.scan(backward, zero_state, (totals, qo_sums), reverse=True)

    def one_block(items):
        query_block, key_block, value_block, grad_block, cumul_block, state_in, adjoint_in = items
        lead, tail = decay_factors(cumul_block)
        return block_terms(query_block, key_block, value_block, grad_block, cumul_block, lead, tail, state_in, adjoint_in)
    d_query, d_key, d_value = lax.map(one_block, (query_heads, key_heads, value_heads, grad_heads, cumulative, states_in, adjoints_in))
    width = ATTENTION_HEADS * HEAD
    d_queries = (scale * d_query).reshape(SEQUENCE_TOKENS, width).astype(jnp.bfloat16)
    d_keys = (scale * d_key).reshape(SEQUENCE_TOKENS, width).astype(jnp.bfloat16)
    d_values = (scale * d_value).reshape(SEQUENCE_TOKENS, width).astype(jnp.bfloat16)
    owners = N_SEQ * N_EXP
    expert_index = expert_ids.reshape(owners, TOK_DEV * 2)
    onehot = (expert_index[:, :, None] == jnp.arange(EXPERTS, dtype=jnp.int32)[None, None, :]).astype(jnp.int32)
    earlier = jnp.cumsum(onehot, axis=1) - onehot
    rank = lax.optimization_barrier(jnp.sum(earlier * onehot, axis=2))
    slots = jnp.arange(owners, dtype=jnp.int32)[:, None] * MOST + rank
    routed = (gate_probs[:, :, None] * upstream[:, None, :].astype(jnp.float32)).astype(jnp.bfloat16).reshape(owners * TOK_DEV * 2, D)
    expert_grad = jnp.zeros((EXPERTS, SLOTS, D), jnp.bfloat16).at[expert_index.reshape(-1), slots.reshape(-1)].set(routed)

    def one_expert(pair):
        saved, gradient = pair
        return jnp.dot(saved, gradient, preferred_element_type=jnp.float32).astype(jnp.bfloat16)
    d_down = lax.map(one_expert, (activations, expert_grad))
    return (d_queries, d_keys, d_values, d_down)
```

```python
import functools
import math

import jax
import jax.numpy as jnp
from jax import lax
from jax.experimental import pallas as pl
from jax.experimental.pallas import tpu as pltpu
from jax.sharding import PartitionSpec as P

HEAD = 128
EXPERTS = 16
MOST = 9
ROWS = 144
ZCH = 4
CH = 8
F32, BF16 = jnp.float32, jnp.bfloat16


def route_kernel(
    up_ref, meta_ref, w_hbm, act_hbm, down_hbm, grad_ref,
    G, upbuf, metabuf, wbuf, actbuf, acc, stage,
    zsend, zrecv, gsend, grecv, lsem, osem,
):
    s, j = lax.axis_index("seq"), lax.axis_index("exp")
    x, y, z, core = s // 4, s % 4, j // 2, j % 2
    width = up_ref.shape[1]
    zw, gw = width // ZCH, width // CH

    def plane(xx, yy):
        return {"seq": (xx % 4) * 4 + yy % 4, "exp": j}

    def column(zz, cc):
        return {"seq": s, "exp": (zz % 4) * 2 + cc}

    zup, zdown, mate = column(z + 1, core), column(z + 3, core), column(z, 1 - core)
    barrier = pltpu.get_barrier_semaphore()
    for peer in (plane(x + 1, y), plane(x + 3, y), plane(x, y + 1), plane(x, y + 3), zup, zdown, mate):
        pl.semaphore_signal(barrier, inc=1, device_id=peer, device_id_type=pl.DeviceIdType.MESH)

    wcopy = pltpu.make_async_copy(w_hbm, wbuf, lsem.at[0])
    acopy = pltpu.make_async_copy(act_hbm, actbuf, lsem.at[1])
    wcopy.start()
    acopy.start()
    own = [pltpu.make_async_copy(meta_ref, metabuf.at[j], lsem.at[2])] + [
        pltpu.make_async_copy(up_ref.at[:, k * zw : (k + 1) * zw], upbuf.at[k, j], lsem.at[3 + k])
        for k in range(ZCH)
    ]
    for copy in own:
        copy.start()
    pl.semaphore_wait(barrier, 7)

    def remote(src, dst, ssem, rsem, dev):
        return pltpu.make_async_remote_copy(
            src_ref=src, dst_ref=dst, send_sem=ssem, recv_sem=rsem,
            device_id=dev, device_id_type=pl.DeviceIdType.MESH,
        )

    sent = []

    def zslot(item, slot):
        return metabuf.at[slot] if item == ZCH else upbuf.at[item, slot]

    def zsource(item):
        return meta_ref if item == ZCH else up_ref.at[:, item * zw : (item + 1) * zw]

    def zgo(item, n, src, slot, rn, dev):
        copy = remote(src, zslot(item, slot), zsend.at[item, n], zrecv.at[item, rn], dev)
        copy.start()
        sent.append(copy)

    def zwait(item, rn, slot):
        remote(zslot(item, slot), zslot(item, slot), zsend.at[item, 0], zrecv.at[item, rn], mate).wait_recv()

    def exps(zz, cc):
        return ((zz + 4) % 4) * 2 + cc

    for item in (ZCH, *range(ZCH)):
        zgo(item, 0, zsource(item), j, 0, zup)
        zgo(item, 1, zsource(item), j, 1, zdown)
        zgo(item, 2, zsource(item), j, 3, mate)

    def zforward(item):
        below, above, far = exps(z - 1, core), exps(z + 1, core), exps(z + 2, core)
        zwait(item, 0, below)
        if item % 2 == 0:
            zgo(item, 3, zslot(item, below), below, 2, zup)
        zgo(item, 4, zslot(item, below), below, 4, mate)
        zwait(item, 1, above)
        if item % 2 == 1:
            zgo(item, 3, zslot(item, above), above, 2, zdown)
        zgo(item, 5, zslot(item, above), above, 5, mate)

    def zfinish(item):
        far = exps(z + 2, core)
        zwait(item, 2, far)
        zgo(item, 6, zslot(item, far), far, 6, mate)
        for rn, slot in ((3, exps(z, 1 - core)), (4, exps(z - 1, 1 - core)), (5, exps(z + 1, 1 - core)), (6, exps(z + 2, 1 - core))):
            zwait(item, rn, slot)

    def ring(c):
        if c % 2 == 0:
            return x, y, (lambda d: plane(x + d, y)), (lambda d: plane(x, y + d))
        return y, x, (lambda d: plane(x, y + d)), (lambda d: plane(x + d, y))

    def ggo(c, n, ref, dev):
        copy = remote(ref, ref, gsend.at[c, n], grecv.at[c, n], dev)
        copy.start()
        sent.append(copy)

    def gwait(c, n, ref):
        remote(ref, ref, gsend.at[c, n], grecv.at[c, n], mate).wait_recv()

    def slab(c, a, b):
        return G.at[c, b * 4 + (a + 4) % 4]

    def group(c, b):
        return G.at[c, pl.ds(((b + 4) % 4) * 4, 4)]

    def turn(c):
        return (c // 2) % 2 == 0

    def stage1(c):
        a, b, na, _ = ring(c)
        ggo(c, 0, slab(c, a, b), na(1))
        ggo(c, 1, slab(c, a, b), na(3))

    def stage2(c):
        a, b, na, _ = ring(c)
        if turn(c):
            gwait(c, 0, slab(c, a - 1, b))
            ggo(c, 2, slab(c, a - 1, b), na(1))
            gwait(c, 1, slab(c, a + 1, b))
        else:
            gwait(c, 1, slab(c, a + 1, b))
            ggo(c, 2, slab(c, a + 1, b), na(3))
            gwait(c, 0, slab(c, a - 1, b))

    def stage3(c):
        a, b, _, nb = ring(c)
        gwait(c, 2, slab(c, a + 2, b))
        ggo(c, 3, group(c, b), nb(1))
        ggo(c, 4, group(c, b), nb(3))

    def stage4(c):
        a, b, _, nb = ring(c)
        if turn(c):
            gwait(c, 3, group(c, b - 1))
            ggo(c, 5, group(c, b - 1), nb(1))
            gwait(c, 4, group(c, b + 1))
        else:
            gwait(c, 4, group(c, b + 1))
            ggo(c, 5, group(c, b + 1), nb(3))
            gwait(c, 3, group(c, b - 1))

    outs = []

    def stage5(c):
        a, b, _, _ = ring(c)
        gwait(c, 5, group(c, b + 2))
        if c >= 2:
            outs[c - 2].wait()
        for e in range(2):
            order = [(q % 4) * 4 + q // 4 if c % 2 == 0 else q for q in range(16)]
            rows = jnp.concatenate([G[c, q, e * 72 : (e + 1) * 72, :] for q in order], axis=0)
            stage[c % 2, e] = jnp.dot(actbuf[e], rows, preferred_element_type=F32).astype(BF16)
        out = pltpu.make_async_copy(stage.at[c % 2], down_hbm.at[:, :, c * gw : (c + 1) * gw], osem.at[c % 2])
        out.start()
        outs.append(out)

    for copy in own:
        copy.wait()
    zforward(ZCH)
    zfinish(ZCH)
    row = lax.broadcasted_iota(jnp.int32, (ROWS, 64), 0)
    local = row % 72
    base = (row // 72 + 2 * j) * MOST + local % MOST
    block_of = local // MOST
    picks, gates = [], []
    for t in range(8):
        table = metabuf[t]
        code0, code1 = table[0:1, 0:64], table[1:2, 0:64]
        gate0, gate1 = table[2:3, 0:64], table[3:4, 0:64]
        want = jnp.where(block_of == t, base, -1).astype(F32)
        hit0, hit1 = want == code0, want == code1
        picks.append(jnp.where(hit0 | hit1, 1.0, 0.0))
        gates.append(jnp.sum(jnp.where(hit0, gate0, 0.0) + jnp.where(hit1, gate1, 0.0), axis=1, keepdims=True))
    pick = jnp.concatenate(picks, axis=1).astype(BF16)
    gate = sum(gates)

    def select(c):
        k, off = c // (CH // ZCH), (c % (CH // ZCH)) * gw
        tokens = upbuf[k, :, :, off : off + gw].reshape(512, gw)
        a, b, _, _ = ring(c)
        rows = jnp.dot(pick, tokens, preferred_element_type=F32)
        G[c, b * 4 + a] = (rows * gate).astype(BF16)
        part = lax.dot_general(
            tokens, wbuf[:, c * gw : (c + 1) * gw], (((1,), (1,)), ((), ())), preferred_element_type=F32
        )
        if c == 0:
            acc[...] = part
        else:
            acc[...] += part
        stage1(c)

    per = CH // ZCH
    zforward(0)
    for k in range(ZCH):
        zfinish(k)
        if k + 1 < ZCH:
            zforward(k + 1)
        if k == 0:
            wcopy.wait()
        for c in range(per * k, per * k + per):
            select(c)
        if k >= 1:
            for c in range(per * (k - 1), per * k):
                stage2(c)
            for c in range(per * (k - 1), per * k):
                stage3(c)
    grad_ref[...] = acc[...].astype(BF16)
    for c in range(per * (ZCH - 1), CH):
        stage2(c)
    for c in range(per * (ZCH - 1), CH):
        stage3(c)
    acopy.wait()
    for c in range(CH + 1):
        if c < CH:
            stage4(c)
        if c >= 1:
            stage5(c - 1)
    outs[CH - 2].wait()
    outs[CH - 1].wait()
    for copy in sent:
        copy.wait_send()


def route(upstream, meta, out_weight, activations):
    width = upstream.shape[1]
    gw, zw = width // CH, width // ZCH
    return pl.pallas_call(
        route_kernel,
        out_shape=(
            jax.ShapeDtypeStruct((2, 288, width), BF16),
            jax.ShapeDtypeStruct((512, 512), BF16),
        ),
        in_specs=[
            pl.BlockSpec(memory_space=pltpu.VMEM),
            pl.BlockSpec(memory_space=pltpu.VMEM),
            pl.BlockSpec(memory_space=pl.ANY),
            pl.BlockSpec(memory_space=pl.ANY),
        ],
        out_specs=(pl.BlockSpec(memory_space=pl.ANY), pl.BlockSpec(memory_space=pltpu.VMEM)),
        scratch_shapes=[
            pltpu.VMEM((CH, 16, ROWS, gw), BF16),
            pltpu.VMEM((ZCH, 8, 64, zw), BF16),
            pltpu.VMEM((8, 8, 128), F32),
            pltpu.VMEM((512, width), BF16),
            pltpu.VMEM((2, 288, 1152), BF16),
            pltpu.VMEM((512, 512), F32),
            pltpu.VMEM((2, 2, 288, gw), BF16),
            pltpu.SemaphoreType.DMA((ZCH + 1, 7)),
            pltpu.SemaphoreType.DMA((ZCH + 1, 7)),
            pltpu.SemaphoreType.DMA((CH, 6)),
            pltpu.SemaphoreType.DMA((CH, 6)),
            pltpu.SemaphoreType.DMA((3 + ZCH,)),
            pltpu.SemaphoreType.DMA((2,)),
        ],
        compiler_params=pltpu.CompilerParams(
            collective_id=0, has_side_effects=True, vmem_limit_bytes=64000 * 1024
        ),
        name="route",
    )(upstream, meta, out_weight, activations)


def scan_states(decay, value, backward):
    count, mine = lax.axis_size("seq"), lax.axis_index("seq")
    if backward:
        mine = count - 1 - mine

    def shift(part, d):
        pairs = [(i + d, i) if backward else (i, i + d) for i in range(count - d)]
        return lax.ppermute(part, "seq", pairs)

    factor, value = shift(decay, 1), shift(value, 1)
    factor = jnp.where(mine >= 1, factor, 1.0)
    d = 1
    while d < count - 1:
        other_f, other_v = shift(factor, d), shift(value, d)
        here = mine >= d
        value = value + jnp.where(here, factor[:, None, None] * other_v, 0.0)
        factor = factor * jnp.where(here, other_f, 1.0)
        d *= 2
    return value


def shards(
    upstream, out_weight, queries, keys, values, log_decay, expert_ids, gate_probs, activations
):
    rows_here = queries.shape[0]
    heads_here = queries.shape[1] // HEAD
    scale = 1.0 / math.sqrt(HEAD * rows_here * lax.axis_size("seq"))
    flat = expert_ids.reshape(-1)
    onehot = (flat[:, None] == jnp.arange(EXPERTS, dtype=jnp.int32)[None, :]).astype(F32)
    place = jnp.arange(flat.shape[0])
    before = (place[:, None] > place[None, :]).astype(F32)
    earlier = jnp.dot(before, onehot, preferred_element_type=F32)
    rank = jnp.sum(earlier * onehot, axis=1)
    code = (flat.astype(F32) * MOST + rank).reshape(-1, 2)
    meta = jnp.concatenate([code.T, gate_probs.T], axis=0)
    meta = jnp.pad(meta, ((0, 4), (0, 64)))

    d_down, grad_out = route(upstream, meta, out_weight, activations)

    def split(block):
        return block.reshape(rows_here, heads_here, HEAD).transpose(1, 0, 2)

    q, k, v, o = split(queries), split(keys), split(values), split(grad_out)
    cumulative = jnp.cumsum(log_decay, axis=1)
    lead = jnp.exp(cumulative)[:, :, None]
    tail = jnp.exp(cumulative[:, -1:] - cumulative)[:, :, None]
    decay = jnp.exp(cumulative[:, -1])

    def dot(spec, a, b):
        return jnp.einsum(spec, a, b, preferred_element_type=F32)

    kv_sum = dot("hse,hsf->hef", (k * tail).astype(BF16), v)
    qo_sum = dot("hte,htf->hef", (q * lead).astype(BF16), o)
    state_in = scan_states(decay, kv_sum, False).astype(BF16)
    adjoint_in = scan_states(decay, qo_sum, True).astype(BF16)
    position = jnp.arange(rows_here)
    lower = position[:, None] >= position[None, :]
    spread = cumulative[:, :, None] - cumulative[:, None, :]
    weights = jnp.where(lower[None], jnp.exp(jnp.minimum(spread, 0.0)), 0.0)
    mixed = (dot("htf,hsf->hts", o, v) * weights).astype(BF16)
    paired = (dot("hte,hse->hts", q, k) * weights).astype(BF16)
    d_query = dot("hts,hse->hte", mixed, k) + lead * dot("htf,hef->hte", o, state_in)
    d_key = dot("hts,hte->hse", mixed, q) + tail * dot("hsf,hef->hse", v, adjoint_in)
    d_value = dot("hts,htf->hsf", paired, o) + tail * dot("hse,hef->hsf", k, adjoint_in)

    def join(part):
        return (scale * part).astype(BF16).transpose(1, 0, 2).reshape(rows_here, -1)

    return (join(d_query), join(d_key), join(d_value), d_down)


def solution(mesh):
    return jax.shard_map(
        shards,
        mesh=mesh,
        in_specs=(
            P(("seq", "exp"), None),
            P("exp", None),
            P("seq", "exp"),
            P("seq", "exp"),
            P("seq", "exp"),
            P("exp", "seq"),
            P(("seq", "exp"), None),
            P(("seq", "exp"), None),
            P("exp", "seq", None),
        ),
        out_specs=(P("seq", "exp"), P("seq", "exp"), P("seq", "exp"), P("exp", "seq", None)),
        check_vma=False,
    )
```

```python
import math

import jax
import jax.numpy as jnp
from jax import lax
from jax.experimental import pallas as pl
from jax.experimental.pallas import tpu as pltpu
from jax.sharding import PartitionSpec as P

HEAD = 128
SEQUENCE = 8192
MOST = 9
ROWS = 144
ZCH = 4
CH = 8
F32, BF16 = jnp.float32, jnp.bfloat16


def split(value):
    high = value.astype(BF16)
    return high, (value - high.astype(F32)).astype(BF16)


def dot2(value, other, dims):
    high, low = split(value)
    dims = (dims, ((), ()))
    return lax.dot_general(high, other, dims, preferred_element_type=F32) + lax.dot_general(
        low, other, dims, preferred_element_type=F32
    )


def layer_kernel(
    up_ref, meta_ref, q_ref, k_ref, v_ref, decay_ref, w_hbm, act_hbm,
    down_hbm, dq_ref, dk_ref, dv_ref,
    G, upbuf, metabuf, wbuf, actbuf, acc, stage, grad, tab, colc, rowc, ybuf, xbuf, carry,
    zsend, zrecv, gsend, grecv, ysend, yrecv, xsend, xrecv, lsem, osem,
):
    s, j = lax.axis_index("seq"), lax.axis_index("exp")
    x, y, z, core = s // 4, s % 4, j // 2, j % 2
    width = up_ref.shape[1]
    zw, gw = width // ZCH, width // CH
    scale = 1.0 / math.sqrt(HEAD * SEQUENCE)

    def plane(xx, yy):
        return {"seq": (xx % 4) * 4 + yy % 4, "exp": j}

    def column(zz, cc):
        return {"seq": s, "exp": (zz % 4) * 2 + cc}

    zup, zdown, mate = column(z + 1, core), column(z + 3, core), column(z, 1 - core)
    barrier = pltpu.get_barrier_semaphore()
    for peer in (plane(x + 1, y), plane(x + 3, y), plane(x, y + 1), plane(x, y + 3), zup, zdown, mate):
        pl.semaphore_signal(barrier, inc=1, device_id=peer, device_id_type=pl.DeviceIdType.MESH)

    own = [pltpu.make_async_copy(meta_ref, metabuf.at[j], lsem.at[2])] + [
        pltpu.make_async_copy(up_ref.at[:, k * zw : (k + 1) * zw], upbuf.at[k, j], lsem.at[3 + k])
        for k in range(ZCH)
    ]
    for copy in own:
        copy.start()
    wcopy = pltpu.make_async_copy(w_hbm, wbuf, lsem.at[0])
    acopy = pltpu.make_async_copy(act_hbm, actbuf, lsem.at[1])
    wcopy.start()
    acopy.start()
    pl.semaphore_wait(barrier, 7)

    sent = []

    def send(src, dst, ssem, rsem, dev):
        copy = pltpu.make_async_remote_copy(
            src_ref=src, dst_ref=dst, send_sem=ssem, recv_sem=rsem,
            device_id=dev, device_id_type=pl.DeviceIdType.MESH,
        )
        copy.start()
        sent.append(copy)

    def arrived(ref, ssem, rsem):
        pltpu.make_async_remote_copy(
            src_ref=ref, dst_ref=ref, send_sem=ssem, recv_sem=rsem,
            device_id=mate, device_id_type=pl.DeviceIdType.MESH,
        ).wait_recv()

    def zslot(item, slot):
        return metabuf.at[slot] if item == ZCH else upbuf.at[item, slot]

    def zsource(item):
        return meta_ref if item == ZCH else up_ref.at[:, item * zw : (item + 1) * zw]

    def zgo(item, n, src, slot, rn, dev):
        send(src, zslot(item, slot), zsend.at[item, n], zrecv.at[item, rn], dev)

    def zwait(item, rn, slot):
        arrived(zslot(item, slot), zsend.at[item, 0], zrecv.at[item, rn])

    def exps(zz, cc):
        return ((zz + 4) % 4) * 2 + cc

    for item in (ZCH, *range(ZCH)):
        zgo(item, 0, zsource(item), j, 0, zup)
        zgo(item, 1, zsource(item), j, 1, zdown)
        zgo(item, 2, zsource(item), j, 3, mate)

    def zforward(item):
        below, above = exps(z - 1, core), exps(z + 1, core)
        zwait(item, 0, below)
        if item % 2 == 0:
            zgo(item, 3, zslot(item, below), below, 2, zup)
        zgo(item, 4, zslot(item, below), below, 4, mate)
        zwait(item, 1, above)
        if item % 2 == 1:
            zgo(item, 3, zslot(item, above), above, 2, zdown)
        zgo(item, 5, zslot(item, above), above, 5, mate)

    def zfinish(item):
        far = exps(z + 2, core)
        zwait(item, 2, far)
        zgo(item, 6, zslot(item, far), far, 6, mate)
        for rn, slot in (
            (3, exps(z, 1 - core)),
            (4, exps(z - 1, 1 - core)),
            (5, exps(z + 1, 1 - core)),
            (6, exps(z + 2, 1 - core)),
        ):
            zwait(item, rn, slot)

    def ring(c):
        if c % 2 == 0:
            return x, y, (lambda d: plane(x + d, y)), (lambda d: plane(x, y + d))
        return y, x, (lambda d: plane(x, y + d)), (lambda d: plane(x + d, y))

    def slab(c, a, b):
        place = b * 4 + (a + 4) % 4
        return tab.at[place] if c > CH else G.at[c, place]

    def group(c, b):
        place = pl.ds(((b + 4) % 4) * 4, 4)
        return tab.at[place] if c > CH else G.at[c, place]

    def ggo(c, n, ref, dev):
        send(ref, ref, gsend.at[c, n], grecv.at[c, n], dev)

    def gwait(c, n, ref):
        arrived(ref, gsend.at[c, n], grecv.at[c, n])

    def turn(c):
        return (c // 2) % 2 == 0

    def stage1(c):
        a, b, na, _ = ring(c)
        ggo(c, 0, slab(c, a, b), na(1))
        ggo(c, 1, slab(c, a, b), na(3))

    def stage2(c):
        a, b, na, _ = ring(c)
        if turn(c):
            gwait(c, 0, slab(c, a - 1, b))
            ggo(c, 2, slab(c, a - 1, b), na(1))
            gwait(c, 1, slab(c, a + 1, b))
        else:
            gwait(c, 1, slab(c, a + 1, b))
            ggo(c, 2, slab(c, a + 1, b), na(3))
            gwait(c, 0, slab(c, a - 1, b))

    def stage3(c):
        a, b, _, nb = ring(c)
        gwait(c, 2, slab(c, a + 2, b))
        ggo(c, 3, group(c, b), nb(1))
        ggo(c, 4, group(c, b), nb(3))

    def stage4(c):
        a, b, _, nb = ring(c)
        if turn(c):
            gwait(c, 3, group(c, b - 1))
            ggo(c, 5, group(c, b - 1), nb(1))
            gwait(c, 4, group(c, b + 1))
        else:
            gwait(c, 4, group(c, b + 1))
            ggo(c, 5, group(c, b + 1), nb(3))
            gwait(c, 3, group(c, b - 1))

    outs = []

    def stage5(c):
        a, b, _, _ = ring(c)
        gwait(c, 5, group(c, b + 2))
        if c > CH:
            return
        if c >= 2:
            outs[c - 2].wait()
        for e in range(2):
            order = [(p % 4) * 4 + p // 4 if c % 2 == 0 else p for p in range(16)]
            rows = jnp.concatenate([G[c, p, e * 72 : (e + 1) * 72, :] for p in order], axis=0)
            stage[c % 2, e] = jnp.dot(actbuf[e], rows, preferred_element_type=F32).astype(BF16)
        out = pltpu.make_async_copy(stage.at[c % 2], down_hbm.at[:, :, c * gw : (c + 1) * gw], osem.at[c % 2])
        out.start()
        outs.append(out)

    def states_out(kind, ref, lo):
        for h in range(4):
            cols = slice(h * HEAD, (h + 1) * HEAD)
            c = colc[h]
            factor = jnp.exp(c[511:512, :] - c) if kind == 0 else jnp.exp(c)
            left = ref[:, cols].astype(F32) * factor
            ybuf[kind, y, h] = dot2(left, lo[:, cols], ((0,), (0,))).astype(BF16)

    def ygo(kind):
        send(ybuf.at[kind, y], ybuf.at[kind, y], ysend.at[kind, 0], yrecv.at[kind, 0], plane(x, y + 1))
        send(ybuf.at[kind, y], ybuf.at[kind, y], ysend.at[kind, 1], yrecv.at[kind, 1], plane(x, y + 3))

    def xgo(kind):
        send(xbuf.at[kind, x], xbuf.at[kind, x], xsend.at[kind, 0], xrecv.at[kind, 0], plane(x + 1, y))
        send(xbuf.at[kind, x], xbuf.at[kind, x], xsend.at[kind, 1], xrecv.at[kind, 1], plane(x + 3, y))

    def pass_on(kind, buf, at, ssem, rsem, up, down):
        below, above = buf.at[kind, (at + 3) % 4], buf.at[kind, (at + 1) % 4]
        arrived(below, ssem.at[kind, 0], rsem.at[kind, 0])
        arrived(above, ssem.at[kind, 1], rsem.at[kind, 1])
        if kind == 0:
            send(below, below, ssem.at[kind, 2], rsem.at[kind, 2], up)
        else:
            send(above, above, ssem.at[kind, 2], rsem.at[kind, 2], down)

    def ypass(kind):
        pass_on(kind, ybuf, y, ysend, yrecv, plane(x, y + 1), plane(x, y + 3))

    def xpass(kind):
        pass_on(kind, xbuf, x, xsend, xrecv, plane(x + 1, y), plane(x + 3, y))

    def far(kind, buf, at, ssem, rsem):
        arrived(buf.at[kind, (at + 2) % 4], ssem.at[kind, 2], rsem.at[kind, 2])

    def span(logs, low, high):
        total = jnp.zeros_like(logs[0])
        for r in range(4):
            total = total + jnp.where((r > low) & (r < high), 1.0, 0.0) * logs[r]
        return jnp.exp(total) * jnp.where(low < high, 1.0, 0.0)

    def row_logs():
        return [tab[x * 4 + r] for r in range(4)]

    def mix(coefs, buf, kind, h):
        return sum(coefs[r][h : h + 1, :] * buf[kind, r, h].astype(F32) for r in range(4))

    def states_row(kind):
        far(kind, ybuf, y, ysend, yrecv)
        logs = row_logs()
        coefs = [span(logs, r, 4) if kind == 0 else span(logs, -1, r) for r in range(4)]
        for h in range(4):
            xbuf[kind, x, h] = mix(coefs, ybuf, kind, h).astype(BF16)

    def states_in(kind):
        far(kind, xbuf, x, xsend, xrecv)
        logs = row_logs()
        whole = [sum(tab[q * 4 + r] for r in range(4)) for q in range(4)]
        if kind == 0:
            near = [span(logs, r, y) for r in range(4)]
            rest = span(logs, -1, y)
            wide = [span(whole, q, x) * rest for q in range(4)]
        else:
            near = [span(logs, y, r) for r in range(4)]
            rest = span(logs, y, 4)
            wide = [span(whole, x, q) * rest for q in range(4)]
        for h in range(4):
            total = mix(near, ybuf, kind, h) + mix(wide, xbuf, kind, h)
            high, low = split(total)
            carry[kind, h, 0] = high
            carry[kind, h, 1] = low

    def attention():
        place_t = lax.broadcasted_iota(jnp.int32, (512, 512), 0)
        place_s = lax.broadcasted_iota(jnp.int32, (512, 512), 1)

        def head(h, _):
            cols = pl.ds(pl.multiple_of(h * HEAD, HEAD), HEAD)
            q, k, v, o = q_ref[:, cols], k_ref[:, cols], v_ref[:, cols], grad[:, cols]
            c = colc[h]
            column_c, row_c = jnp.concatenate([c] * 4, axis=1), rowc[h, 0:1, :]
            spread = column_c - row_c
            weight = jnp.where(place_t >= place_s, jnp.exp(jnp.minimum(spread, 0.0)), 0.0)
            flipped = jnp.where(place_t <= place_s, jnp.exp(jnp.minimum(-spread, 0.0)), 0.0)
            lead, tail = jnp.exp(c), jnp.exp(c[511:512, :] - c)

            def outer(one, two):
                return lax.dot_general(one, two, (((1,), (1,)), ((), ())), preferred_element_type=F32)

            def inner(one, two):
                return jnp.dot(one, two, preferred_element_type=F32)

            dq = dot2(outer(o, v) * weight, k, ((1,), (0,)))
            dq = dq + lead * (outer(o, carry[0, h, 0]) + outer(o, carry[0, h, 1]))
            dq_ref[:, cols] = (scale * dq).astype(BF16)
            dk = dot2(outer(v, o) * flipped, q, ((1,), (0,)))
            dk = dk + tail * (outer(v, carry[1, h, 0]) + outer(v, carry[1, h, 1]))
            dk_ref[:, cols] = (scale * dk).astype(BF16)
            dv = dot2(outer(k, q) * flipped, o, ((1,), (0,)))
            dv = dv + tail * (inner(k, carry[1, h, 0]) + inner(k, carry[1, h, 1]))
            dv_ref[:, cols] = (scale * dv).astype(BF16)
            return 0

        lax.fori_loop(0, 4, head, 0)

    logs = decay_ref[...]
    tab[s] = jnp.broadcast_to(jnp.sum(logs, axis=1, keepdims=True), (8, HEAD))
    low = lax.broadcasted_iota(jnp.int32, (512, 512), 0) >= lax.broadcasted_iota(jnp.int32, (512, 512), 1)
    sums = jnp.where(low, 1.0, 0.0).astype(BF16)
    part, rest = [], logs
    for _ in range(3):
        part.append(rest.astype(BF16))
        rest = rest - part[-1].astype(F32)
    for h in range(4):
        colc[h] = sum(
            lax.dot_general(
                sums, jnp.broadcast_to(p[h : h + 1, :], (HEAD, 512)), (((1,), (1,)), ((), ())),
                preferred_element_type=F32,
            )
            for p in part
        )
        rowc[h] = sum(
            lax.dot_general(
                jnp.broadcast_to(p[h : h + 1, :], (8, 512)), sums, (((1,), (1,)), ((), ())),
                preferred_element_type=F32,
            )
            for p in part
        )
    states_out(0, k_ref, v_ref)
    stage1(CH + 1)
    ygo(0)

    for copy in own:
        copy.wait()
    zforward(ZCH)
    zforward(0)
    zfinish(ZCH)
    row = lax.broadcasted_iota(jnp.int32, (ROWS, 64), 0)
    local = row % 72
    expert = (row // 72 + 2 * j).astype(F32)
    second, want, block_of = row // 72 == 1, (local % MOST).astype(F32), local // MOST
    ahead = lax.broadcasted_iota(jnp.int32, (64, 64), 0) < lax.broadcasted_iota(jnp.int32, (64, 64), 1)
    ahead = jnp.where(ahead, 1.0, 0.0).astype(BF16)
    which = (lax.broadcasted_iota(jnp.int32, (8, 64), 0) + 2 * j).astype(F32)
    picks, gates = [], []
    for t in range(8):
        table = metabuf[t]
        name0, name1 = table[0:1, 0:64], table[1:2, 0:64]
        gate0, gate1 = table[2:3, 0:64], table[3:4, 0:64]
        named = jnp.where((which == name0) | (which == name1), 1.0, 0.0)
        rank = jnp.dot(named.astype(BF16), ahead, preferred_element_type=F32)
        right = (jnp.where(second, rank[1:2, :], rank[0:1, :]) == want) & (block_of == t)
        hit0, hit1 = right & (name0 == expert), right & (name1 == expert)
        picks.append(jnp.where(hit0 | hit1, 1.0, 0.0))
        gates.append(jnp.sum(jnp.where(hit0, gate0, 0.0) + jnp.where(hit1, gate1, 0.0), axis=1, keepdims=True))
    pick = jnp.concatenate(picks, axis=1).astype(BF16)
    gate = sum(gates)

    def select(c):
        k, off = c // (CH // ZCH), (c % (CH // ZCH)) * gw
        tokens = upbuf[k, :, :, off : off + gw].reshape(512, gw)
        a, b, _, _ = ring(c)
        rows = jnp.dot(pick, tokens, preferred_element_type=F32)
        G[c, b * 4 + a] = (rows * gate).astype(BF16)
        part = lax.dot_general(
            tokens, wbuf[:, c * gw : (c + 1) * gw], (((1,), (1,)), ((), ())), preferred_element_type=F32
        )
        if c == 0:
            acc[...] = part
        else:
            acc[...] += part
        stage1(c)

    per = CH // ZCH
    for k in range(ZCH):
        zfinish(k)
        if k + 1 < ZCH:
            zforward(k + 1)
        if k == 0:
            wcopy.wait()
        for c in range(per * k, per * k + per):
            select(c)
        if k == 0:
            stage2(CH + 1)
            stage3(CH + 1)
            ypass(0)
        if k == 1:
            stage2(0), stage2(1), stage3(0), stage3(1)
            stage4(CH + 1)
            states_row(0)
            xgo(0)
        if k == 2:
            stage2(2), stage2(3)
            xpass(0)
        if k == 3:
            stage3(2), stage3(3)
            stage2(4), stage2(5)
    grad[...] = acc[...].astype(BF16)
    states_out(1, q_ref, grad)
    stage2(6), stage2(7)
    ygo(1)
    stage4(0), stage4(1)
    stage3(4), stage3(5)
    ypass(1)
    stage5(CH + 1)
    states_in(0)
    stage4(2), stage4(3)
    stage3(6), stage3(7)
    states_row(1)
    acopy.wait()
    xgo(1)
    stage5(0), stage5(1)
    stage4(4), stage4(5)
    xpass(1)
    stage4(6), stage4(7)
    states_in(1)
    attention()
    for c in range(2, CH):
        stage5(c)
    outs[CH - 2].wait()
    outs[CH - 1].wait()
    for copy in sent:
        copy.wait_send()


def layer(upstream, meta, queries, keys, values, decays, out_weight, activations):
    width = upstream.shape[1]
    gw, zw = width // CH, width // ZCH
    here = pl.BlockSpec(memory_space=pltpu.VMEM)
    there = pl.BlockSpec(memory_space=pl.ANY)
    small = jax.ShapeDtypeStruct((512, 512), BF16)
    return pl.pallas_call(
        layer_kernel,
        out_shape=(jax.ShapeDtypeStruct((2, 288, width), BF16), small, small, small),
        in_specs=[here] * 6 + [there] * 2,
        out_specs=(there, here, here, here),
        scratch_shapes=[
            pltpu.VMEM((CH, 16, ROWS, gw), BF16),
            pltpu.VMEM((ZCH, 8, 64, zw), BF16),
            pltpu.VMEM((8, 8, 128), F32),
            pltpu.VMEM((512, width), BF16),
            pltpu.VMEM((2, 288, 1152), BF16),
            pltpu.VMEM((512, 512), F32),
            pltpu.VMEM((2, 2, 288, gw), BF16),
            pltpu.VMEM((512, 512), BF16),
            pltpu.VMEM((16, 8, HEAD), F32),
            pltpu.VMEM((4, 512, HEAD), F32),
            pltpu.VMEM((4, 8, 512), F32),
            pltpu.VMEM((2, 4, 4, HEAD, HEAD), BF16),
            pltpu.VMEM((2, 4, 4, HEAD, HEAD), BF16),
            pltpu.VMEM((2, 4, 2, HEAD, HEAD), BF16),
            pltpu.SemaphoreType.DMA((ZCH + 1, 7)),
            pltpu.SemaphoreType.DMA((ZCH + 1, 7)),
            pltpu.SemaphoreType.DMA((CH + 2, 6)),
            pltpu.SemaphoreType.DMA((CH + 2, 6)),
            pltpu.SemaphoreType.DMA((2, 3)),
            pltpu.SemaphoreType.DMA((2, 3)),
            pltpu.SemaphoreType.DMA((2, 3)),
            pltpu.SemaphoreType.DMA((2, 3)),
            pltpu.SemaphoreType.DMA((3 + ZCH,)),
            pltpu.SemaphoreType.DMA((2,)),
        ],
        compiler_params=pltpu.CompilerParams(
            collective_id=0, has_side_effects=True, vmem_limit_bytes=64000 * 1024
        ),
        name="layer",
    )(upstream, meta, queries, keys, values, decays, out_weight, activations)


def shards(
    upstream, out_weight, queries, keys, values, log_decay, expert_ids, gate_probs, activations
):
    meta = jnp.concatenate([expert_ids.astype(F32).T, gate_probs.T], axis=0)
    meta = jnp.pad(meta, ((0, 4), (0, 64)))
    decays = jnp.pad(log_decay, ((0, 4), (0, 0)))
    d_down, d_queries, d_keys, d_values = layer(
        upstream, meta, queries, keys, values, decays, out_weight, activations
    )
    return (d_queries, d_keys, d_values, d_down)


def solution(mesh):
    return jax.shard_map(
        shards,
        mesh=mesh,
        in_specs=(
            P(("seq", "exp"), None),
            P("exp", None),
            P("seq", "exp"),
            P("seq", "exp"),
            P("seq", "exp"),
            P("exp", "seq"),
            P(("seq", "exp"), None),
            P(("seq", "exp"), None),
            P("exp", "seq", None),
        ),
        out_specs=(P("seq", "exp"), P("seq", "exp"), P("seq", "exp"), P("exp", "seq", None)),
        check_vma=False,
    )
```
